256 devices in a mesh: dp: 8 (over x, core), graph: 32 (over z, y).
Axes of the slice: x: 4, y: 4, z: 8, core: 2. Of those that a mesh axis runs over, the one named last changes fastest.
Arguments:
- feats: bfloat16 [8, 16384, 512], P('dp', 'graph'), may hold values from -6 to 6
- grad_out: bfloat16 [8, 16384, 512], P('dp', 'graph'), may hold values from -6 to 6
- w_self: bfloat16 [512, 512], replicated, may hold values from -0.25 to 0.25
- w_neigh: bfloat16 [512, 512], replicated, may hold values from -0.25 to 0.25
- nbr: int32 [8, 16384, 10], P('dp', 'graph'), may hold values from 0 to 2047, as said below
- deg: int32 [8, 16384], P('dp', 'graph'), may hold values from 1 to 10
- hub_rows: int32 [8, 512], P('dp', 'graph'), may hold values from 0 to 511, as said below
- send_rows: int32 [8, 32, 32, 32], P('dp', 'graph'), may hold values from 0 to 511
Outputs:
- out: bfloat16 [8, 16384, 512], P('dp', 'graph')
- grad_feats: bfloat16 [8, 16384, 512], P('dp', 'graph')
- grad_w_self: float32 [512, 512], P('graph')
- grad_w_neigh: float32 [512, 512], P('graph')
The draws below stay inside these ranges and needn't reach their ends.
Inputs may be any that keep to these rules, and one draw needn't show every extreme that they name: `hub_rows`: within each partition's block of 16 entries the rows are distinct rows of that partition. `nbr`: entries name rows of the partition's table: below 512 its own rows, then 512 hub rows, then 1024 received rows. Only slots below deg are live.
All inputs are finite; a program needn't handle non-finite values.
Results may differ from the reference program's by a relative error of at most 0.007.
Values may be sent and summed in bfloat16 or wider, within the bound.
A program may use at most 64 MiB of HBM per device.

```python
import jax
import jax.numpy as jnp
from jax import lax

F = 512
V_DEV = 512
H_DEV = 16
CAP = 32
K = 10
PARTS_SIZE = 32
BATCHES = 8
VERTS = 16384
HUBS = 512
RECV = 1024


def draw_nbr(key, part):
    keys = jax.random.split(key, 4)
    shape = (BATCHES, VERTS, K)
    kinds = jax.random.randint(keys[0], shape, 0, 10)
    local_idx = jax.random.randint(keys[1], shape, 0, V_DEV)
    hub_idx = V_DEV + jax.random.randint(keys[2], shape, 0, HUBS)
    recv_idx = V_DEV + HUBS + jax.random.randint(keys[3], shape, 0, RECV)
    return jnp.where(kinds < 4, local_idx, jnp.where(kinds < 7, hub_idx, recv_idx)).astype(jnp.int32)


def draw_hub_rows(key, part):
    blocks = BATCHES * (HUBS // H_DEV)
    keys = jax.random.split(key, blocks)
    picked = jax.vmap(lambda k: jax.random.permutation(k, V_DEV)[:H_DEV])(keys)
    return picked.reshape(BATCHES, HUBS).astype(jnp.int32)


def place_ends(drawn, rng, least, largest):
    spot = [jax.random.randint(jax.random.fold_in(rng, axis), (), 0, length) for axis, length in enumerate(drawn.shape)]
    main_axis = drawn.shape.index(max(drawn.shape))
    next_to = spot[:main_axis] + [(spot[main_axis] + 1) % drawn.shape[main_axis]] + spot[main_axis + 1:]
    return drawn.at[tuple(spot)].set(least).at[tuple(next_to)].set(largest)


def block_levels(key, dims, cuts, least, high):
    gain = 1.0
    for axis_at, blocks in cuts:
        draws = jax.random.uniform(jax.random.fold_in(jax.random.fold_in(key, 6), axis_at), (blocks,), jnp.float32, least / len(cuts), high / len(cuts))
        gain = gain * jnp.repeat(jnp.exp(draws), dims[axis_at] // blocks).reshape((-1,) + (1,) * (len(dims) - 1 - axis_at))
    return gain


def normal_values(stream_key, dims, scale, limit, cuts=(), held_as=jnp.bfloat16):
    loudness = block_levels(stream_key, dims, cuts, -0.22, 0.18) if cuts else 1.0
    values = jax.random.normal(stream_key, dims, jnp.float32) * scale * loudness
    return jnp.minimum(jnp.maximum(values, -limit), limit).astype(held_as)


def setup_inputs(seed: int = 0) -> dict:
    streams_of = jax.random.split(jax.random.key(seed), 9)
    return {
        "feats": normal_values(streams_of[0], (BATCHES, VERTS, F), 1.0, 6.0, ((0, 8), (1, 32))),
        "grad_out": normal_values(streams_of[1], (BATCHES, VERTS, F), 1.0, 6.0, ((0, 8), (1, 32))),
        "w_self": normal_values(streams_of[2], (F, F), F ** -0.5, 0.25),
        "w_neigh": normal_values(streams_of[3], (F, F), F ** -0.5, 0.25),
        "nbr": draw_nbr(jax.random.fold_in(streams_of[8], 71), 0),
        "deg": place_ends(jax.random.randint(streams_of[5], (BATCHES, VERTS), 1, K + 1), jax.random.fold_in(streams_of[5], 1), 1, K).astype(jnp.int32),
        "hub_rows": draw_hub_rows(jax.random.fold_in(streams_of[8], 71), 0),
        "send_rows": place_ends(jax.random.randint(streams_of[7], (BATCHES, PARTS_SIZE, PARTS_SIZE, CAP), 0, V_DEV), jax.random.fold_in(streams_of[7], 1), 0, V_DEV - 1).astype(jnp.int32),
    }


def part_work(own, table, idx, dcount, grads, w_self, w_neigh, nhub):
    rows, width = own.shape
    slots = idx.shape[1]
    live = jnp.arange(slots)[None, :] < dcount[:, None]
    total = jnp.zeros((rows, width), jnp.float32)
    for k in range(slots):
        total = total + jnp.where(live[:, k:k + 1], table[idx[:, k]].astype(jnp.float32), 0.0)
    degree = dcount.astype(jnp.float32)[:, None]
    agg = (total / degree).astype(jnp.bfloat16)
    result = (jnp.dot(own, w_self, preferred_element_type=jnp.float32) + jnp.dot(agg, w_neigh, preferred_element_type=jnp.float32)).astype(jnp.bfloat16)
    trans = (((1,), (1,)), ((), ()))
    back = lax.dot_general(grads, w_neigh, trans, preferred_element_type=jnp.float32) / degree
    height = table.shape[0]
    dtable = jnp.zeros((height, width), jnp.float32)
    for k in range(slots):
        target = jnp.where(live[:, k], idx[:, k], height)
        dtable = dtable.at[target].add(back, mode='drop')
    dlocal = lax.dot_general(grads, w_self, trans, preferred_element_type=jnp.float32) + dtable[:rows]
    inner = (((0,), (0,)), ((), ()))
    dws = lax.dot_general(own, grads, inner, preferred_element_type=jnp.float32)
    dwn = lax.dot_general(agg, grads, inner, preferred_element_type=jnp.float32)
    return (result, dlocal, dtable[rows:rows + nhub], dtable[rows + nhub:], dws, dwn)

def reference(feats, grad_out, w_self, w_neigh, nbr, deg, hub_rows, send_rows):
    parts = PARTS_SIZE
    rows = feats.shape[1] // parts
    width = feats.shape[2]
    slots = nbr.shape[2]
    slot_cap = send_rows.shape[-1]

    def per_batch(item):
        fb, gb, nb, db, hb, sb = item
        fb = fb.reshape(parts, rows, width)
        gb = gb.reshape(parts, rows, width)
        nb = nb.reshape(parts, rows, slots)
        db = db.reshape(parts, rows)
        hb = hb.reshape(parts, -1)
        hubs = jax.vmap(lambda f, r: f[r])(fb, hb).reshape(-1, width)
        nhub = hubs.shape[0]

        def per_part(p):
            own = fb[p]
            recv = jax.vmap(lambda f, r: f[r])(fb, sb[:, p]).reshape(-1, width)
            table = jnp.concatenate([own, hubs, recv], axis=0)
            res, dlocal, dhub, drecv, dws, dwn = part_work(own, table, nb[p], db[p], gb[p], w_self, w_neigh, nhub)
            return (res, dlocal, dhub, drecv.reshape(parts, slot_cap, width), dws, dwn)
        res, dlocal, dhub, drecv, dws, dwn = lax.map(per_part, jnp.arange(parts, dtype=jnp.int32))
        hub_total = lax.optimization_barrier(jnp.sum(dhub, axis=0)).reshape(parts, -1, width)

        def finish(q):
            grad_rows = dlocal[q].at[hb[q]].add(hub_total[q])
            grad_rows = grad_rows.at[sb[q].reshape(-1)].add(drecv[:, q].reshape(-1, width))
            return grad_rows.astype(jnp.bfloat16)
        grad_rows = lax.map(finish, jnp.arange(parts, dtype=jnp.int32))
        return (res.reshape(-1, width), grad_rows.reshape(-1, width), lax.optimization_barrier(jnp.sum(dws, axis=0)), lax.optimization_barrier(jnp.sum(dwn, axis=0)))
    res, grad_rows, dws, dwn = lax.map(per_batch, (feats, grad_out, nbr, deg, hub_rows, send_rows))
    scale = 1.0 / jnp.sqrt(jnp.float32(feats.shape[0] * feats.shape[1]))
    return (res, grad_rows, lax.optimization_barrier(jnp.sum(dws, axis=0)) * scale, lax.optimization_barrier(jnp.sum(dwn, axis=0)) * scale)
```

```python
import functools

import jax
import jax.numpy as jnp
from jax import lax
from jax.experimental import pallas as pl
from jax.experimental.pallas import tpu as pltpu
from jax.sharding import PartitionSpec as P

F32 = jnp.float32
BF16 = jnp.bfloat16
TRANS = (((1,), (1,)), ((), ()))
INNER = (((0,), (0,)), ((), ()))


def dot(a, b, dims=(((1,), (0,)), ((), ()))):
    return lax.dot_general(a, b, dims, preferred_element_type=F32)


def layer_kernel(
    parts,
    groups,
    scale,
    own_ref,
    g_ref,
    ws_ref,
    wn_ref,
    nbr_ref,
    deg_ref,
    idx_ref,
    out_ref,
    gf_ref,
    gws_ref,
    gwn_ref,
    live_ref,
    pick_ref,
    spread_ref,
    count_t_ref,
    count_ref,
    send_ref,
    hub_ref,
    recv_ref,
    hubs_ref,
    hi_ref,
    lo_ref,
    dlocal_ref,
    back_send_ref,
    back_hub_ref,
    back_recv_ref,
    back_hubs_ref,
    base_ref,
    agg_ref,
    inv_ref,
    dw_ref,
    dw_recv_ref,
    slab_ref,
    slab_recv_ref,
    fin_ref,
    fin_recv_ref,
    f_send,
    f_recv,
    fh_send,
    fh_recv,
    b_send,
    b_recv,
    bh_send,
    bh_recv,
    w_send,
    w_recv,
    s_send,
    s_recv,
    e_send,
    e_recv,
):
    rows, width = own_ref.shape
    slots = nbr_ref.shape[0]
    cap = recv_ref.shape[0] // parts
    hub = hubs_ref.shape[0] // parts
    sent = recv_ref.shape[0]
    lanes = 128
    me = lax.axis_index("graph")
    lane = lax.axis_index("dp")
    height = count_t_ref.shape[0]

    def graph_peer(k):
        return lax.rem(me + k, parts)

    def dp_peer(k):
        return lax.rem(lane + k, groups)

    barrier = pltpu.get_barrier_semaphore()

    @pl.loop(1, parts)
    def _(k):
        pl.semaphore_signal(barrier, inc=1, device_id={"graph": graph_peer(k)})

    @pl.loop(1, groups)
    def _(k):
        pl.semaphore_signal(barrier, inc=1, device_id={"dp": dp_peer(k)})

    def column(row, n=lanes):
        return jnp.transpose(jnp.broadcast_to(row, (n, lanes)))

    lane_iota = lax.broadcasted_iota(jnp.int32, (lanes, lanes), 1)
    for i in range(sent // lanes + 1):
        spot = column(idx_ref[i : i + 1, :])
        tall = lanes if i < sent // lanes else hub
        for j in range(width // lanes):
            hit = (spot == lane_iota + lanes * j).astype(F32).astype(BF16)
            pick_ref[lanes * i : lanes * i + tall, lanes * j : lanes * (j + 1)] = hit[:tall]
    for i in range(sent // 256):
        send_ref[256 * i : 256 * (i + 1), :] = dot(
            pick_ref[256 * i : 256 * (i + 1), :], own_ref[...]
        ).astype(BF16)
    hub_ref[...] = dot(pick_ref[sent : sent + hub, :], own_ref[...]).astype(BF16)

    pl.semaphore_wait(barrier, parts - 1 + groups - 1)

    def exchange(k, src, dst, ssem, rsem, size, shared):
        q = graph_peer(k)
        return pltpu.make_async_remote_copy(
            src_ref=src if shared else src.at[pl.ds(pl.multiple_of(q * size, size), size)],
            dst_ref=dst.at[pl.ds(pl.multiple_of(me * size, size), size)],
            send_sem=ssem.at[k],
            recv_sem=rsem.at[k],
            device_id={"graph": q},
        )

    def arrival(k, dst, ssem, rsem, size):
        q = lax.rem(me + parts - k, parts)
        spot = dst.at[pl.ds(pl.multiple_of(q * size, size), size)]
        return pltpu.make_async_remote_copy(
            src_ref=spot,
            dst_ref=spot,
            send_sem=ssem.at[k],
            recv_sem=rsem.at[k],
            device_id={"graph": graph_peer(k)},
        )

    @pl.loop(1, parts)
    def _(k):
        exchange(k, send_ref, recv_ref, f_send, f_recv, cap, False).start()
        exchange(k, hub_ref, hubs_ref, fh_send, fh_recv, hub, True).start()

    recv_ref[pl.ds(pl.multiple_of(me * cap, cap), cap), :] = send_ref[
        pl.ds(pl.multiple_of(me * cap, cap), cap), :
    ]
    hubs_ref[pl.ds(pl.multiple_of(me * hub, hub), hub), :] = hub_ref[...]

    def put_dw(m, lhs_ref):
        for b in range(width // lanes):
            part = dot(lhs_ref[...], g_ref[:, lanes * b : lanes * (b + 1)], INNER)
            part = part.reshape(parts, 2, 8, lanes)
            for a in range(2):
                dw_ref[m, 4 * a + b] = part[:, a]

    def dw_copy(k, m):
        p = dp_peer(k)
        return pltpu.make_async_remote_copy(
            src_ref=dw_ref.at[m, p],
            dst_ref=dw_recv_ref.at[m, lane],
            send_sem=w_send.at[m, k],
            recv_sem=w_recv.at[m, k],
            device_id={"dp": p},
        )

    def dw_arrival(k, m):
        p = lax.rem(lane + groups - k, groups)
        spot = dw_recv_ref.at[m, p]
        return pltpu.make_async_remote_copy(
            src_ref=spot,
            dst_ref=spot,
            send_sem=w_send.at[m, k],
            recv_sem=w_recv.at[m, k],
            device_id={"dp": dp_peer(k)},
        )

    for k in range(slots):
        live_ref[k : k + 1, :] = jnp.where(
            deg_ref[...] > k, nbr_ref[k : k + 1, :], -1
        )
    for i in range(rows // lanes):
        inv_ref[lanes * i : lanes * (i + 1), :] = column(
            1.0 / deg_ref[:, lanes * i : lanes * (i + 1)].astype(F32)
        )
    tall = 32
    row_iota = lax.broadcasted_iota(jnp.int32, (tall, rows), 0)

    @pl.loop(0, height // tall)
    def _(i):
        total = jnp.zeros((tall, rows), F32)
        spot = row_iota + i * tall
        for k in range(slots):
            total = total + jnp.where(live_ref[k : k + 1, :] == spot, 1.0, 0.0)
        count_t_ref[pl.ds(pl.multiple_of(i * tall, tall), tall), :] = total.astype(BF16)

    step = 128

    @pl.loop(0, rows // step)
    def _(i):
        span = pl.ds(pl.multiple_of(i * step, step), step)
        inv = inv_ref[span, :]
        back = dot(g_ref[span, :], wn_ref[...], TRANS) * jnp.concatenate([inv] * 4, axis=1)
        hi = back.astype(BF16)
        hi_ref[span, :] = hi
        lo_ref[span, :] = (back - hi.astype(F32)).astype(BF16)

    def dtable(start):
        c = count_t_ref[pl.ds(pl.multiple_of(start, step), step), :]
        return dot(c, hi_ref[...]) + dot(c, lo_ref[...])

    @pl.loop(0, sent // step)
    def _(i):
        span = pl.ds(pl.multiple_of(i * step, step), step)
        back_send_ref[span, :] = dtable(2 * rows + i * step).astype(BF16)

    @pl.loop(0, rows // step)
    def _(i):
        span = pl.ds(pl.multiple_of(i * step, step), step)
        back_hub_ref[span, :] = dtable(rows + i * step).astype(BF16)

    @pl.loop(1, parts)
    def _(k):
        exchange(k, back_send_ref, back_recv_ref, b_send, b_recv, cap, False).start()
        exchange(k, back_hub_ref, back_hubs_ref, bh_send, bh_recv, hub, False).start()

    back_recv_ref[pl.ds(pl.multiple_of(me * cap, cap), cap), :] = back_send_ref[
        pl.ds(pl.multiple_of(me * cap, cap), cap), :
    ]
    back_hubs_ref[pl.ds(pl.multiple_of(me * hub, hub), hub), :] = back_hub_ref[
        pl.ds(pl.multiple_of(me * hub, hub), hub), :
    ]

    put_dw(0, own_ref)

    @pl.loop(1, groups)
    def _(k):
        dw_copy(k, 0).start()

    @pl.loop(0, rows // step)
    def _(i):
        span = pl.ds(pl.multiple_of(i * step, step), step)
        dlocal_ref[span, :] = dtable(i * step) + dot(g_ref[span, :], ws_ref[...], TRANS)
        base_ref[span, :] = dot(own_ref[span, :], ws_ref[...])

    for i in range(height // lanes):
        count_ref[:, lanes * i : lanes * (i + 1)] = jnp.transpose(
            count_t_ref[lanes * i : lanes * (i + 1), :]
        )

    down = lax.broadcasted_iota(jnp.int32, (rows, lanes), 0)
    for i in range(sent // lanes + 1):
        spread_ref[:, lanes * i : lanes * (i + 1)] = (
            (idx_ref[i : i + 1, :] == down).astype(F32).astype(BF16)
        )

    @pl.loop(1, parts)
    def _(k):
        arrival(k, recv_ref, f_send, f_recv, cap).wait_recv()
        arrival(k, hubs_ref, fh_send, fh_recv, hub).wait_recv()

    @pl.loop(0, rows // step)
    def _(i):
        span = pl.ds(pl.multiple_of(i * step, step), step)
        total = dot(count_ref[span, :rows], own_ref[...])
        total = total + dot(count_ref[span, rows : 2 * rows], hubs_ref[...])
        total = total + dot(count_ref[span, 2 * rows :], recv_ref[...])
        agg_ref[span, :] = (total * jnp.concatenate([inv_ref[span, :]] * 4, axis=1)).astype(BF16)

    put_dw(1, agg_ref)

    @pl.loop(1, groups)
    def _(k):
        dw_copy(k, 1).start()

    @pl.loop(0, rows // step)
    def _(i):
        span = pl.ds(pl.multiple_of(i * step, step), step)
        out_ref[span, :] = (base_ref[span, :] + dot(agg_ref[span, :], wn_ref[...])).astype(BF16)

    for m in range(2):

        @pl.loop(1, groups)
        def _(k):
            dw_arrival(k, m).wait_recv()

        dw_recv_ref[m, lane] = dw_ref[m, lane]

        @pl.loop(0, parts)
        def _(q):
            total = dw_recv_ref[m, 0, q]
            for p in range(1, groups):
                total = total + dw_recv_ref[m, p, q]
            slab_ref[q, m] = total

    def slab_copy(k):
        q = graph_peer(k)
        return pltpu.make_async_remote_copy(
            src_ref=slab_ref.at[q],
            dst_ref=slab_recv_ref.at[me],
            send_sem=s_send.at[k],
            recv_sem=s_recv.at[k],
            device_id={"graph": q},
        )

    def slab_arrival(k):
        spot = slab_recv_ref.at[lax.rem(me + parts - k, parts)]
        return pltpu.make_async_remote_copy(
            src_ref=spot,
            dst_ref=spot,
            send_sem=s_send.at[k],
            recv_sem=s_recv.at[k],
            device_id={"graph": graph_peer(k)},
        )

    @pl.loop(1, parts)
    def _(k):
        slab_copy(k).start()

    slab_recv_ref[me] = slab_ref[me]

    @pl.loop(1, parts)
    def _(k):
        arrival(k, back_recv_ref, b_send, b_recv, cap).wait_recv()
        arrival(k, back_hubs_ref, bh_send, bh_recv, hub).wait_recv()

    @pl.loop(0, rows // step)
    def _(i):
        span = pl.ds(pl.multiple_of(i * step, step), step)
        total = dlocal_ref[span, :] + dot(spread_ref[span, :sent], back_recv_ref[...])
        tail = spread_ref[span, sent:]
        for j in range(parts * hub // lanes):
            total = total + dot(tail, back_hubs_ref[lanes * j : lanes * (j + 1), :])
        gf_ref[span, :] = total.astype(BF16)

    @pl.loop(1, parts)
    def _(k):
        slab_arrival(k).wait_recv()

    for m in range(2):
        total = slab_recv_ref[0, m]
        for q in range(1, parts):
            total = total + slab_recv_ref[q, m]
        fin_ref[m] = total * scale

    def fin_copy(k):
        p = dp_peer(k)
        return pltpu.make_async_remote_copy(
            src_ref=fin_ref,
            dst_ref=fin_recv_ref.at[lane],
            send_sem=e_send.at[k],
            recv_sem=e_recv.at[k],
            device_id={"dp": p},
        )

    def fin_arrival(k):
        spot = fin_recv_ref.at[lax.rem(lane + groups - k, groups)]
        return pltpu.make_async_remote_copy(
            src_ref=spot,
            dst_ref=spot,
            send_sem=e_send.at[k],
            recv_sem=e_recv.at[k],
            device_id={"dp": dp_peer(k)},
        )

    @pl.loop(1, groups)
    def _(k):
        fin_copy(k).start()

    fin_recv_ref[lane] = fin_ref[...]

    @pl.loop(1, groups)
    def _(k):
        fin_arrival(k).wait_recv()

    for a in range(2):
        for b in range(width // lanes):
            here = (slice(8 * a, 8 * (a + 1)), slice(lanes * b, lanes * (b + 1)))
            gws_ref[here] = fin_recv_ref[4 * a + b, 0]
            gwn_ref[here] = fin_recv_ref[4 * a + b, 1]

    @pl.loop(1, parts)
    def _(k):
        exchange(k, send_ref, recv_ref, f_send, f_recv, cap, False).wait_send()
        exchange(k, hub_ref, hubs_ref, fh_send, fh_recv, hub, True).wait_send()
        exchange(k, back_send_ref, back_recv_ref, b_send, b_recv, cap, False).wait_send()
        exchange(k, back_hub_ref, back_hubs_ref, bh_send, bh_recv, hub, False).wait_send()
        slab_copy(k).wait_send()

    @pl.loop(1, groups)
    def _(k):
        dw_copy(k, 0).wait_send()
        dw_copy(k, 1).wait_send()
        fin_copy(k).wait_send()


def shards(feats, grad_out, w_self, w_neigh, nbr, deg, hub_rows, send_rows):
    own = feats[0]
    rows, width = own.shape
    slots = nbr.shape[2]
    parts = lax.axis_size("graph")
    groups = lax.axis_size("dp")
    hub = hub_rows.shape[1]
    cap = send_rows.shape[3]
    sent = parts * cap
    nhub = parts * hub
    height = rows + nhub + sent
    idx = jnp.concatenate(
        [send_rows.reshape(sent // 128, 128), jnp.tile(hub_rows, (1, 128 // hub))], axis=0
    )
    scale = float((groups * parts * rows) ** -0.5)
    vmem = pltpu.VMEM
    dma = pltpu.SemaphoreType.DMA
    outs = pl.pallas_call(
        functools.partial(layer_kernel, parts, groups, scale),
        out_shape=(
            jax.ShapeDtypeStruct((rows, width), BF16),
            jax.ShapeDtypeStruct((rows, width), BF16),
            jax.ShapeDtypeStruct((width // parts, width), F32),
            jax.ShapeDtypeStruct((width // parts, width), F32),
        ),
        in_specs=[pl.BlockSpec(memory_space=vmem)] * 7,
        out_specs=[pl.BlockSpec(memory_space=vmem)] * 4,
        scratch_shapes=[
            vmem((slots, rows), jnp.int32),
            vmem((sent + hub, rows), BF16),
            vmem((rows, sent + 128), BF16),
            vmem((height, rows), BF16),
            vmem((rows, height), BF16),
            vmem((sent, width), BF16),
            vmem((hub, width), BF16),
            vmem((sent, width), BF16),
            vmem((nhub, width), BF16),
            vmem((rows, width), BF16),
            vmem((rows, width), BF16),
            vmem((rows, width), F32),
            vmem((sent, width), BF16),
            vmem((nhub, width), BF16),
            vmem((sent, width), BF16),
            vmem((nhub, width), BF16),
            vmem((rows, width), F32),
            vmem((rows, width), BF16),
            vmem((rows, 128), F32),
            vmem((2, groups, parts, 8, 128), F32),
            vmem((2, groups, parts, 8, 128), F32),
            vmem((parts, 2, 8, 128), F32),
            vmem((parts, 2, 8, 128), F32),
            vmem((2, 8, 128), F32),
            vmem((groups, 2, 8, 128), F32),
        ]
        + [dma((parts,))] * 8
        + [dma((2, groups))] * 2
        + [dma((parts,))] * 2
        + [dma((groups,))] * 2,
        compiler_params=pltpu.CompilerParams(collective_id=0, has_side_effects=True),
    )(own, grad_out[0], w_self, w_neigh, nbr[0].T, deg, idx)
    out, grad_feats, grad_w_self, grad_w_neigh = outs
    return (out[None], grad_feats[None], grad_w_self, grad_w_neigh)


def solution(mesh):
    placed = (
        P("dp", "graph", None),
        P("dp", "graph", None),
        P(),
        P(),
        P("dp", "graph", None),
        P("dp", "graph"),
        P("dp", "graph"),
        P("dp", "graph", None, None),
    )
    return jax.shard_map(
        shards,
        mesh=mesh,
        in_specs=placed,
        out_specs=(
            P("dp", "graph", None),
            P("dp", "graph", None),
            P("graph", None),
            P("graph", None),
        ),
        check_vma=False,
    )
```

```python
import functools

import jax
import jax.numpy as jnp
from jax import lax
from jax.experimental import pallas as pl
from jax.experimental.pallas import tpu as pltpu
from jax.sharding import PartitionSpec as P

F32 = jnp.float32
BF16 = jnp.bfloat16
COLUMNS = 4
TRANS = (((1,), (1,)), ((), ()))


def dot(a, b, dims=(((1,), (0,)), ((), ()))):
    return lax.dot_general(a, b, dims, preferred_element_type=F32)


def layer_kernel(
    parts,
    groups,
    scale,
    own_ref,
    g_ref,
    ws_ref,
    wn_ref,
    nbr_ref,
    deg_ref,
    rows_ref,
    hub_rows_ref,
    out_ref,
    gf_ref,
    gws_ref,
    gwn_ref,
    idx_ref,
    live_ref,
    pick_ref,
    spread_ref,
    count_t_ref,
    count_ref,
    send_ref,
    hub_ref,
    recv_ref,
    hubs_ref,
    hi_ref,
    lo_ref,
    grad_ref,
    back_send_ref,
    back_hub_ref,
    back_recv_ref,
    back_slab_ref,
    back_sum_ref,
    back_hubs_ref,
    base_ref,
    total_ref,
    agg_ref,
    inv_ref,
    dw_ref,
    dw_recv_ref,
    slab_ref,
    slab_recv_ref,
    ring_ref,
    ring_recv_ref,
    fin_ref,
    fin_recv_ref,
    f_send,
    f_recv,
    b_send,
    b_recv,
    hz_send,
    hz_recv,
    hy_send,
    hy_recv,
    ty_send,
    ty_recv,
    tz_send,
    tz_recv,
    w_send,
    w_recv,
    sy_send,
    sy_recv,
    sz_send,
    sz_recv,
    e_send,
    e_recv,
):
    rows, width = own_ref.shape
    slots = nbr_ref.shape[0]
    cap = recv_ref.shape[0] // parts
    hub = hub_ref.shape[0]
    sent = recv_ref.shape[0]
    nhub = hubs_ref.shape[0]
    height = count_t_ref.shape[0]
    ny = COLUMNS
    nz = parts // ny
    lanes = 128
    step = 128
    me = lax.axis_index("graph")
    lane = lax.axis_index("dp")
    z, y = me // ny, lax.rem(me, ny)

    def at(base, size):
        return pl.ds(pl.multiple_of(base * size, size), size)

    def peer(k, sign=1):
        dz, dy = k // ny, lax.rem(k, ny)
        return lax.rem(z + nz + sign * dz, nz) * ny + lax.rem(y + ny + sign * dy, ny)

    def z_at(k):
        return lax.rem(z + k + nz, nz)

    def y_at(k):
        return lax.rem(y + k + ny, ny)

    def d_at(k):
        return lax.rem(lane + k + groups, groups)

    def remote(src, dst, ssem, rsem, device):
        return pltpu.make_async_remote_copy(
            src_ref=src, dst_ref=dst, send_sem=ssem, recv_sem=rsem, device_id=device
        )

    def to_z(k, src, dst, ssem, rsem):
        return remote(src, dst, ssem.at[k], rsem.at[k], {"graph": z_at(k) * ny + y})

    def to_y(k, src, dst, ssem, rsem):
        return remote(src, dst, ssem.at[k], rsem.at[k], {"graph": z * ny + y_at(k)})

    def to_all(k, src, dst, ssem, rsem):
        return remote(src, dst, ssem.at[k], rsem.at[k], {"graph": peer(k)})

    barrier = pltpu.get_barrier_semaphore()

    @pl.loop(1, parts)
    def _(k):
        pl.semaphore_signal(barrier, inc=1, device_id={"graph": peer(k)})

    @pl.loop(1, groups)
    def _(k):
        pl.semaphore_signal(barrier, inc=1, device_id={"dp": d_at(k)})

    per = lanes // cap
    for i in range(sent // lanes):
        idx_ref[i : i + 1, :] = jnp.concatenate(
            [rows_ref[per * i + c : per * i + c + 1, :] for c in range(per)], axis=1
        )
    last = sent // lanes
    idx_ref[last : last + 1, :] = jnp.concatenate([hub_rows_ref[...]] * (lanes // hub), axis=1)

    def column(row):
        return jnp.transpose(jnp.broadcast_to(row, (lanes, lanes)))

    lane_iota = lax.broadcasted_iota(jnp.int32, (lanes, lanes), 1)
    for i in (last, *range(last)):
        spot = column(idx_ref[i : i + 1, :])
        tall = lanes if i < last else hub
        for j in range(width // lanes):
            hit = (spot == lane_iota + lanes * j).astype(F32).astype(BF16)
            pick_ref[lanes * i : lanes * i + tall, lanes * j : lanes * (j + 1)] = hit[:tall]
    hub_ref[...] = dot(pick_ref[sent : sent + hub, :], own_ref[...]).astype(BF16)
    hubs_ref[at(y * nz + z, hub), :] = hub_ref[...]
    for i in range(sent // 256):
        send_ref[256 * i : 256 * (i + 1), :] = dot(
            pick_ref[256 * i : 256 * (i + 1), :], own_ref[...]
        ).astype(BF16)

    pl.semaphore_wait(barrier, parts - 1 + groups - 1)

    def hub_z(k):
        return to_z(k, hub_ref, hubs_ref.at[at(y * nz + z, hub)], hz_send, hz_recv)

    def hub_z_in(k):
        spot = hubs_ref.at[at(y * nz + z_at(-k), hub)]
        return to_z(k, spot, spot, hz_send, hz_recv)

    def hub_y(k):
        spot = hubs_ref.at[at(y, nz * hub)]
        return to_y(k, spot, spot, hy_send, hy_recv)

    def hub_y_in(k):
        spot = hubs_ref.at[at(y_at(-k), nz * hub)]
        return to_y(k, spot, spot, hy_send, hy_recv)

    def forth(k):
        return to_all(
            k, send_ref.at[at(peer(k), cap)], recv_ref.at[at(me, cap)], f_send, f_recv
        )

    def forth_in(k):
        spot = recv_ref.at[at(peer(k, -1), cap)]
        return to_all(k, spot, spot, f_send, f_recv)

    def back(k):
        return to_all(
            k, back_send_ref.at[at(peer(k), cap)], back_recv_ref.at[at(me, cap)], b_send, b_recv
        )

    def back_in(k):
        spot = back_recv_ref.at[at(peer(k, -1), cap)]
        return to_all(k, spot, spot, b_send, b_recv)

    @pl.loop(1, nz)
    def _(k):
        hub_z(k).start()

    @pl.loop(1, parts)
    def _(k):
        forth(k).start()

    recv_ref[at(me, cap), :] = send_ref[at(me, cap), :]

    for k in range(slots):
        name = nbr_ref[k]
        h = name - rows
        moved = rows + ((h // hub) % ny) * (nz * hub) + (h // (hub * ny)) * hub + h % hub
        name = jnp.where((h >= 0) & (h < nhub), moved, name)
        live_ref[k : k + 1, :] = jnp.where(deg_ref[...] > k, name, -1)
    for i in range(rows // lanes):
        inv_ref[lanes * i : lanes * (i + 1), :] = column(
            1.0 / deg_ref[:, lanes * i : lanes * (i + 1)].astype(F32)
        )
    tall = 32
    row_iota = lax.broadcasted_iota(jnp.int32, (tall, rows), 0)

    @pl.loop(0, height // tall)
    def _(i):
        total = jnp.zeros((tall, rows), F32)
        spot = row_iota + i * tall
        for k in range(slots):
            total = total + jnp.where(live_ref[k : k + 1, :] == spot, 1.0, 0.0)
        count_t_ref[at(i, tall), :] = total.astype(BF16)

    @pl.loop(1, nz)
    def _(k):
        hub_z_in(k).wait_recv()

    @pl.loop(1, ny)
    def _(k):
        hub_y(k).start()

    def by_vertex(span):
        return jnp.concatenate([inv_ref[span, :]] * (width // lanes), axis=1)

    @pl.loop(0, rows // step)
    def _(i):
        span = at(i, step)
        term = dot(g_ref[span, :], wn_ref[...], TRANS) * by_vertex(span)
        hi = term.astype(BF16)
        hi_ref[span, :] = hi
        lo_ref[span, :] = (term - hi.astype(F32)).astype(BF16)

    def dtable(start):
        c = count_t_ref[pl.ds(pl.multiple_of(start, step), step), :]
        return dot(c, hi_ref[...]) + dot(c, lo_ref[...])

    @pl.loop(0, nhub // step)
    def _(i):
        back_hub_ref[at(i, step), :] = dtable(rows + i * step).astype(BF16)

    def term_y(k):
        return to_y(
            k, back_hub_ref.at[at(y_at(k), nz * hub)], back_slab_ref.at[y], ty_send, ty_recv
        )

    def term_y_in(k):
        spot = back_slab_ref.at[y_at(-k)]
        return to_y(k, spot, spot, ty_send, ty_recv)

    def term_z(k):
        return to_z(
            k, back_sum_ref.at[at(z_at(k), hub)], back_hubs_ref.at[at(z, hub)], tz_send, tz_recv
        )

    def term_z_in(k):
        spot = back_hubs_ref.at[at(z_at(-k), hub)]
        return to_z(k, spot, spot, tz_send, tz_recv)

    @pl.loop(1, ny)
    def _(k):
        term_y(k).start()

    @pl.loop(0, sent // step)
    def _(i):
        back_send_ref[at(i, step), :] = dtable(rows + nhub + i * step).astype(BF16)

    @pl.loop(1, parts)
    def _(k):
        back(k).start()

    back_recv_ref[at(me, cap), :] = back_send_ref[at(me, cap), :]
    back_slab_ref[y] = back_hub_ref[at(y, nz * hub), :]

    def put_dw(m, lhs_ref):
        own16 = step // 16

        @pl.loop(0, width // step)
        def _(i):
            lhs = jnp.transpose(lhs_ref[:, at(i, step)])
            part = dot(lhs, g_ref[...]).reshape(own16, 2, 8, width)
            for b in range(width // lanes):
                for a in range(2):
                    dw_ref[m, 4 * a + b, at(i, own16)] = part[
                        :, a, :, lanes * b : lanes * (b + 1)
                    ]

    def dw_copy(k, m):
        p = d_at(k)
        return remote(
            dw_ref.at[m, p], dw_recv_ref.at[m, lane], w_send.at[m, k], w_recv.at[m, k], {"dp": p}
        )

    def dw_in(k, m):
        spot = dw_recv_ref.at[m, d_at(-k)]
        return remote(spot, spot, w_send.at[m, k], w_recv.at[m, k], {"dp": d_at(k)})

    put_dw(0, own_ref)

    @pl.loop(1, groups)
    def _(k):
        dw_copy(k, 0).start()

    @pl.loop(1, ny)
    def _(k):
        term_y_in(k).wait_recv()

    total = back_slab_ref[0].astype(F32)
    for k in range(1, ny):
        total = total + back_slab_ref[k].astype(F32)
    back_sum_ref[...] = total.astype(BF16)

    @pl.loop(1, nz)
    def _(k):
        term_z(k).start()

    back_hubs_ref[at(z, hub), :] = back_sum_ref[at(z, hub), :]

    for i in range(height // lanes):
        count_ref[:, lanes * i : lanes * (i + 1)] = jnp.transpose(
            count_t_ref[lanes * i : lanes * (i + 1), :]
        )

    @pl.loop(0, rows // step)
    def _(i):
        span = at(i, step)
        grad_ref[span, :] = dtable(i * step) + dot(g_ref[span, :], ws_ref[...], TRANS)
        base_ref[span, :] = dot(own_ref[span, :], ws_ref[...])
        total_ref[span, :] = dot(count_ref[span, :rows], own_ref[...])

    down = lax.broadcasted_iota(jnp.int32, (rows, lanes), 0)
    for i in range(last + 1):
        spread_ref[:, lanes * i : lanes * (i + 1)] = (
            (idx_ref[i : i + 1, :] == down).astype(F32).astype(BF16)
        )

    @pl.loop(1, ny)
    def _(k):
        hub_y_in(k).wait_recv()

    @pl.loop(0, rows // step)
    def _(i):
        span = at(i, step)
        total_ref[span, :] += dot(count_ref[span, rows : rows + nhub], hubs_ref[...])

    near = [0]
    for k in range(1, nz // 2):
        near += [k, nz - k]
    near.append(nz // 2)
    plane = ny * cap
    for dz in near:

        @pl.loop(max(dz * ny, 1), (dz + 1) * ny)
        def _(k):
            forth_in(k).wait_recv()

        src = z_at(-dz)

        @pl.loop(0, rows // step)
        def _(i):
            span = at(i, step)
            c = count_ref[span, pl.ds(pl.multiple_of(rows + nhub + src * plane, plane), plane)]
            total = total_ref[span, :] + dot(c, recv_ref[at(src, plane), :])
            if dz != near[-1]:
                total_ref[span, :] = total
            else:
                agg_ref[span, :] = (total * by_vertex(span)).astype(BF16)

    put_dw(1, agg_ref)

    @pl.loop(1, groups)
    def _(k):
        dw_copy(k, 1).start()

    @pl.loop(0, rows // step)
    def _(i):
        span = at(i, step)
        out_ref[span, :] = (base_ref[span, :] + dot(agg_ref[span, :], wn_ref[...])).astype(BF16)

    for m in range(2):

        @pl.loop(1, groups)
        def _(k):
            dw_in(k, m).wait_recv()

        dw_recv_ref[m, lane] = dw_ref[m, lane]

        @pl.loop(0, parts)
        def _(q):
            total = dw_recv_ref[m, 0, q]
            for p in range(1, groups):
                total = total + dw_recv_ref[m, p, q]
            slab_ref[lax.rem(q, ny), q // ny, m] = total

    def slab_y(k):
        return to_y(k, slab_ref.at[y_at(k)], slab_recv_ref.at[y], sy_send, sy_recv)

    def slab_y_in(k):
        spot = slab_recv_ref.at[y_at(-k)]
        return to_y(k, spot, spot, sy_send, sy_recv)

    def ring(k):
        return to_z(k, ring_ref.at[z_at(k)], ring_recv_ref.at[z], sz_send, sz_recv)

    def ring_in(k):
        spot = ring_recv_ref.at[z_at(-k)]
        return to_z(k, spot, spot, sz_send, sz_recv)

    @pl.loop(1, ny)
    def _(k):
        slab_y(k).start()

    slab_recv_ref[y] = slab_ref[y]

    @pl.loop(1, ny)
    def _(k):
        slab_y_in(k).wait_recv()

    @pl.loop(0, nz)
    def _(q):
        total = slab_recv_ref[0, q]
        for p in range(1, ny):
            total = total + slab_recv_ref[p, q]
        ring_ref[q] = total

    @pl.loop(1, nz)
    def _(k):
        ring(k).start()

    ring_recv_ref[z] = ring_ref[z]

    @pl.loop(1, nz)
    def _(k):
        term_z_in(k).wait_recv()

    @pl.loop(0, rows // step)
    def _(i):
        span = at(i, step)
        grad_ref[span, :] += dot(spread_ref[span, sent:], back_hubs_ref[...])

    def finish_weights():
        @pl.loop(1, nz)
        def _(k):
            ring_in(k).wait_recv()

        total = ring_recv_ref[0]
        for q in range(1, nz):
            total = total + ring_recv_ref[q]
        fin_ref[...] = total * scale
        fin_recv_ref[lane] = fin_ref[...]

        @pl.loop(1, groups)
        def _(k):
            fin(k).start()

    def fin(k):
        return remote(
            fin_ref, fin_recv_ref.at[lane], e_send.at[k], e_recv.at[k], {"dp": d_at(k)}
        )

    def fin_in(k):
        spot = fin_recv_ref.at[d_at(-k)]
        return remote(spot, spot, e_send.at[k], e_recv.at[k], {"dp": d_at(k)})

    for dz in near:

        @pl.loop(max(dz * ny, 1), (dz + 1) * ny)
        def _(k):
            back_in(k).wait_recv()

        if dz == near[-1]:
            finish_weights()
        src = z_at(-dz)

        @pl.loop(0, rows // step)
        def _(i):
            span = at(i, step)
            c = spread_ref[span, at(src, plane)]
            total = grad_ref[span, :] + dot(c, back_recv_ref[at(src, plane), :])
            if dz != near[-1]:
                grad_ref[span, :] = total
            else:
                gf_ref[span, :] = total.astype(BF16)

    @pl.loop(1, groups)
    def _(k):
        fin_in(k).wait_recv()

    for a in range(2):
        for b in range(width // lanes):
            here = (slice(8 * a, 8 * (a + 1)), slice(lanes * b, lanes * (b + 1)))
            gws_ref[here] = fin_recv_ref[4 * a + b, 0]
            gwn_ref[here] = fin_recv_ref[4 * a + b, 1]

    @pl.loop(1, parts)
    def _(k):
        forth(k).wait_send()
        back(k).wait_send()

    @pl.loop(1, nz)
    def _(k):
        hub_z(k).wait_send()
        term_z(k).wait_send()
        ring(k).wait_send()

    @pl.loop(1, ny)
    def _(k):
        hub_y(k).wait_send()
        term_y(k).wait_send()
        slab_y(k).wait_send()

    @pl.loop(1, groups)
    def _(k):
        dw_copy(k, 0).wait_send()
        dw_copy(k, 1).wait_send()
        fin(k).wait_send()


def shards(feats, grad_out, w_self, w_neigh, nbr, deg, hub_rows, send_rows):
    own = feats[0]
    rows, width = own.shape
    slots = nbr.shape[2]
    parts = lax.axis_size("graph")
    groups = lax.axis_size("dp")
    hub = hub_rows.shape[1]
    cap = send_rows.shape[3]
    sent = parts * cap
    nhub = parts * hub
    height = rows + nhub + sent
    ny = COLUMNS
    nz = parts // ny
    scale = float((groups * parts * rows) ** -0.5)
    vmem = pltpu.VMEM
    dma = pltpu.SemaphoreType.DMA
    outs = pl.pallas_call(
        functools.partial(layer_kernel, parts, groups, scale),
        out_shape=(
            jax.ShapeDtypeStruct((rows, width), BF16),
            jax.ShapeDtypeStruct((rows, width), BF16),
            jax.ShapeDtypeStruct((width // parts, width), F32),
            jax.ShapeDtypeStruct((width // parts, width), F32),
        ),
        in_specs=[pl.BlockSpec(memory_space=vmem)] * 8,
        out_specs=[pl.BlockSpec(memory_space=vmem)] * 4,
        scratch_shapes=[
            vmem((sent // 128 + 1, 128), jnp.int32),
            vmem((slots, rows), jnp.int32),
            vmem((sent + hub, rows), BF16),
            vmem((rows, sent + 128), BF16),
            vmem((height, rows), BF16),
            vmem((rows, height), BF16),
            vmem((sent, width), BF16),
            vmem((hub, width), BF16),
            vmem((sent, width), BF16),
            vmem((nhub, width), BF16),
            vmem((rows, width), BF16),
            vmem((rows, width), BF16),
            vmem((rows, width), F32),
            vmem((sent, width), BF16),
            vmem((nhub, width), BF16),
            vmem((sent, width), BF16),
            vmem((ny, nz * hub, width), BF16),
            vmem((nz * hub, width), BF16),
            vmem((nz * hub, width), BF16),
            vmem((rows, width), F32),
            vmem((rows, width), F32),
            vmem((rows, width), BF16),
            vmem((rows, 128), F32),
            vmem((2, groups, parts, 8, 128), F32),
            vmem((2, groups, parts, 8, 128), F32),
            vmem((ny, nz, 2, 8, 128), F32),
            vmem((ny, nz, 2, 8, 128), F32),
            vmem((nz, 2, 8, 128), F32),
            vmem((nz, 2, 8, 128), F32),
            vmem((2, 8, 128), F32),
            vmem((groups, 2, 8, 128), F32),
        ]
        + [dma((parts,))] * 4
        + ([dma((nz,))] * 2 + [dma((ny,))] * 2)
        + ([dma((ny,))] * 2 + [dma((nz,))] * 2)
        + [dma((2, groups))] * 2
        + ([dma((ny,))] * 2 + [dma((nz,))] * 2)
        + [dma((groups,))] * 2,
        compiler_params=pltpu.CompilerParams(collective_id=0, has_side_effects=True),
    )(
        own,
        grad_out[0],
        w_self,
        w_neigh,
        jnp.transpose(nbr, (2, 0, 1)),
        deg,
        send_rows[0, 0],
        hub_rows,
    )
    out, grad_feats, grad_w_self, grad_w_neigh = outs
    return (out[None], grad_feats[None], grad_w_self, grad_w_neigh)


def solution(mesh):
    placed = (
        P("dp", "graph", None),
        P("dp", "graph", None),
        P(),
        P(),
        P("dp", "graph", None),
        P("dp", "graph"),
        P("dp", "graph"),
        P("dp", "graph", None, None),
    )
    return jax.shard_map(
        shards,
        mesh=mesh,
        in_specs=placed,
        out_specs=(
            P("dp", "graph", None),
            P("dp", "graph", None),
            P("graph", None),
            P("graph", None),
        ),
        check_vma=False,
    )
```

```python
import functools

import jax
import jax.numpy as jnp
from jax import lax
from jax.experimental import pallas as pl
from jax.experimental.pallas import tpu as pltpu
from jax.sharding import PartitionSpec as P

F32 = jnp.float32
BF16 = jnp.bfloat16
COLUMNS = 4
TRANS = (((1,), (1,)), ((), ()))


def dot(a, b, dims=(((1,), (0,)), ((), ()))):
    return lax.dot_general(a, b, dims, preferred_element_type=F32)


def layer_kernel(
    parts,
    groups,
    scale,
    own_hbm,
    g_hbm,
    ws_hbm,
    wn_hbm,
    nbr_hbm,
    deg_hbm,
    rows_hbm,
    hub_rows_hbm,
    out_ref,
    gf_ref,
    gws_ref,
    gwn_ref,
    own_ref,
    g_ref,
    ws_ref,
    wn_ref,
    nbr_ref,
    deg_ref,
    rows_ref,
    hub_rows_ref,
    idx_ref,
    live_ref,
    pick_ref,
    spread_ref,
    count_t_ref,
    count_ref,
    send_ref,
    hub_ref,
    recv_ref,
    hubs_ref,
    hi_ref,
    lo_ref,
    grad_ref,
    back_send_ref,
    back_hub_ref,
    back_recv_ref,
    back_slab_ref,
    back_sum_ref,
    back_hubs_ref,
    base_ref,
    total_ref,
    agg_ref,
    inv_ref,
    dw_ref,
    pair_ref,
    dw_recv_ref,
    slab_ref,
    slab_recv_ref,
    ring_ref,
    ring_recv_ref,
    fin_ref,
    fin_recv_ref,
    load,
    f_send,
    f_recv,
    b_send,
    b_recv,
    hz_send,
    hz_recv,
    hy_send,
    hy_recv,
    ty_send,
    ty_recv,
    tz_send,
    tz_recv,
    p_send,
    p_recv,
    w_send,
    w_recv,
    sy_send,
    sy_recv,
    sz_send,
    sz_recv,
    e_send,
    e_recv,
):
    rows, width = own_ref.shape
    slots = nbr_ref.shape[0]
    cap = recv_ref.shape[0] // parts
    hub = hub_ref.shape[0]
    sent = recv_ref.shape[0]
    nhub = hubs_ref.shape[0]
    height = count_t_ref.shape[0]
    ny = COLUMNS
    nz = parts // ny
    lanes = 128
    step = 256
    me = lax.axis_index("graph")
    lane = lax.axis_index("dp")
    z, y = me // ny, lax.rem(me, ny)

    def at(base, size):
        return pl.ds(pl.multiple_of(base * size, size), size)

    def peer(k, sign=1):
        dz, dy = k // ny, lax.rem(k, ny)
        return lax.rem(z + nz + sign * dz, nz) * ny + lax.rem(y + ny + sign * dy, ny)

    def z_at(k):
        return lax.rem(z + k + nz, nz)

    def y_at(k):
        return lax.rem(y + k + ny, ny)

    def d_at(k):
        return lax.rem(lane + k + groups, groups)

    def remote(src, dst, ssem, rsem, device):
        return pltpu.make_async_remote_copy(
            src_ref=src, dst_ref=dst, send_sem=ssem, recv_sem=rsem, device_id=device
        )

    def to_z(k, src, dst, ssem, rsem):
        return remote(src, dst, ssem.at[k], rsem.at[k], {"graph": z_at(k) * ny + y})

    def to_y(k, src, dst, ssem, rsem):
        return remote(src, dst, ssem.at[k], rsem.at[k], {"graph": z * ny + y_at(k)})

    def to_all(k, src, dst, ssem, rsem):
        return remote(src, dst, ssem.at[k], rsem.at[k], {"graph": peer(k)})

    barrier = pltpu.get_barrier_semaphore()

    @pl.loop(1, parts)
    def _(k):
        pl.semaphore_signal(barrier, inc=1, device_id={"graph": peer(k)})

    @pl.loop(1, groups)
    def _(k):
        pl.semaphore_signal(barrier, inc=1, device_id={"dp": d_at(k)})

    wanted = (
        (rows_hbm, rows_ref),
        (hub_rows_hbm, hub_rows_ref),
        (own_hbm, own_ref),
        (nbr_hbm, nbr_ref),
        (deg_hbm, deg_ref),
        (g_hbm, g_ref),
        (wn_hbm, wn_ref),
        (ws_hbm, ws_ref),
    )
    loads = [
        pltpu.make_async_copy(src, dst, load.at[i]) for i, (src, dst) in enumerate(wanted)
    ]
    for copy in loads:
        copy.start()
    for copy in loads[:3]:
        copy.wait()

    per = lanes // cap
    for i in range(sent // lanes):
        idx_ref[i : i + 1, :] = jnp.concatenate(
            [rows_ref[per * i + c : per * i + c + 1, :] for c in range(per)], axis=1
        )
    last = sent // lanes
    idx_ref[last : last + 1, :] = jnp.concatenate([hub_rows_ref[...]] * (lanes // hub), axis=1)

    def column(row):
        return jnp.transpose(jnp.broadcast_to(row, (lanes, lanes)))

    lane_iota = lax.broadcasted_iota(jnp.int32, (lanes, lanes), 1)
    for i in (last, *range(last)):
        spot = column(idx_ref[i : i + 1, :])
        tall = lanes if i < last else hub
        for j in range(width // lanes):
            hit = (spot == lane_iota + lanes * j).astype(F32).astype(BF16)
            pick_ref[lanes * i : lanes * i + tall, lanes * j : lanes * (j + 1)] = hit[:tall]
    hub_ref[...] = dot(pick_ref[sent : sent + hub, :], own_ref[...]).astype(BF16)
    hubs_ref[at(y * nz + z, hub), :] = hub_ref[...]
    for i in range(sent // 256):
        send_ref[256 * i : 256 * (i + 1), :] = dot(
            pick_ref[256 * i : 256 * (i + 1), :], own_ref[...]
        ).astype(BF16)

    pl.semaphore_wait(barrier, parts - 1 + groups - 1)

    def hub_z(k):
        return to_z(k, hub_ref, hubs_ref.at[at(y * nz + z, hub)], hz_send, hz_recv)

    def hub_z_in(k):
        spot = hubs_ref.at[at(y * nz + z_at(-k), hub)]
        return to_z(k, spot, spot, hz_send, hz_recv)

    def hub_y(k):
        spot = hubs_ref.at[at(y, nz * hub)]
        return to_y(k, spot, spot, hy_send, hy_recv)

    def hub_y_in(k):
        spot = hubs_ref.at[at(y_at(-k), nz * hub)]
        return to_y(k, spot, spot, hy_send, hy_recv)

    def forth(k):
        return to_all(
            k, send_ref.at[at(peer(k), cap)], recv_ref.at[at(me, cap)], f_send, f_recv
        )

    def forth_in(k):
        spot = recv_ref.at[at(peer(k, -1), cap)]
        return to_all(k, spot, spot, f_send, f_recv)

    def back(k):
        return to_all(
            k, back_send_ref.at[at(peer(k), cap)], back_recv_ref.at[at(me, cap)], b_send, b_recv
        )

    def back_in(k):
        spot = back_recv_ref.at[at(peer(k, -1), cap)]
        return to_all(k, spot, spot, b_send, b_recv)

    @pl.loop(1, nz)
    def _(k):
        hub_z(k).start()

    @pl.loop(1, parts)
    def _(k):
        forth(k).start()

    recv_ref[at(me, cap), :] = send_ref[at(me, cap), :]

    for copy in loads[3:]:
        copy.wait()

    for k in range(slots):
        name = nbr_ref[k]
        h = name - rows
        moved = rows + ((h // hub) % ny) * (nz * hub) + (h // (hub * ny)) * hub + h % hub
        name = jnp.where((h >= 0) & (h < nhub), moved, name)
        live_ref[k : k + 1, :] = jnp.where(deg_ref[...] > k, name, -1)
    for i in range(rows // lanes):
        inv_ref[lanes * i : lanes * (i + 1), :] = column(
            1.0 / deg_ref[:, lanes * i : lanes * (i + 1)].astype(F32)
        )
    tall = 32
    row_iota = lax.broadcasted_iota(jnp.int32, (tall, rows), 0)

    @pl.loop(0, height // tall)
    def _(i):
        total = jnp.zeros((tall, rows), F32)
        spot = row_iota + i * tall
        for k in range(slots):
            total = total + jnp.where(live_ref[k : k + 1, :] == spot, 1.0, 0.0)
        count_t_ref[at(i, tall), :] = total.astype(BF16)

    @pl.loop(1, nz)
    def _(k):
        hub_z_in(k).wait_recv()

    @pl.loop(1, ny)
    def _(k):
        hub_y(k).start()

    def by_vertex(span):
        return jnp.concatenate([inv_ref[span, :]] * (width // lanes), axis=1)

    @pl.loop(0, rows // step)
    def _(i):
        span = at(i, step)
        term = dot(g_ref[span, :], wn_ref[...], TRANS) * by_vertex(span)
        hi = term.astype(BF16)
        hi_ref[span, :] = hi
        lo_ref[span, :] = (term - hi.astype(F32)).astype(BF16)

    def dtable(start):
        c = count_t_ref[pl.ds(pl.multiple_of(start, step), step), :]
        return dot(c, hi_ref[...]) + dot(c, lo_ref[...])

    @pl.loop(0, nhub // step)
    def _(i):
        back_hub_ref[at(i, step), :] = dtable(rows + i * step).astype(BF16)

    def term_y(k):
        return to_y(
            k, back_hub_ref.at[at(y_at(k), nz * hub)], back_slab_ref.at[y], ty_send, ty_recv
        )

    def term_y_in(k):
        spot = back_slab_ref.at[y_at(-k)]
        return to_y(k, spot, spot, ty_send, ty_recv)

    def term_z(k):
        return to_z(
            k, back_sum_ref.at[at(z_at(k), hub)], back_hubs_ref.at[at(z, hub)], tz_send, tz_recv
        )

    def term_z_in(k):
        spot = back_hubs_ref.at[at(z_at(-k), hub)]
        return to_z(k, spot, spot, tz_send, tz_recv)

    @pl.loop(1, ny)
    def _(k):
        term_y(k).start()

    @pl.loop(0, sent // step)
    def _(i):
        back_send_ref[at(i, step), :] = dtable(rows + nhub + i * step).astype(BF16)

    @pl.loop(1, parts)
    def _(k):
        back(k).start()

    back_recv_ref[at(me, cap), :] = back_send_ref[at(me, cap), :]
    back_slab_ref[y] = back_hub_ref[at(y, nz * hub), :]

    def put_dw(m, lhs_ref):
        own16 = lanes // 16

        @pl.loop(0, width // lanes)
        def _(i):
            lhs = jnp.transpose(lhs_ref[:, at(i, lanes)])
            part = dot(lhs, g_ref[...]).reshape(own16, 2, 8, width)
            for b in range(width // lanes):
                for a in range(2):
                    dest = 4 * a + b
                    dw_ref[m, dest % 2, dest // 2, at(i, own16)] = part[
                        :, a, :, lanes * b : lanes * (b + 1)
                    ]

    nx = groups // 2
    core = lax.rem(lane, 2)
    x = lane // 2

    def x_at(k):
        return lax.rem(x + k + nx, nx)

    def pair(m):
        return remote(
            dw_ref.at[m, 1 - core],
            pair_ref.at[m],
            p_send.at[m],
            p_recv.at[m],
            {"dp": 2 * x + 1 - core},
        )

    def pair_sum(m):
        pair(m).wait_recv()

        @pl.loop(0, nx)
        def _(q):
            pair_ref[m, q] += dw_ref[m, core, q]

        @pl.loop(1, nx)
        def _(k):
            dw_copy(k, m).start()

        dw_recv_ref[m, x] = pair_ref[m, x]

    def dw_copy(k, m):
        return remote(
            pair_ref.at[m, x_at(k)],
            dw_recv_ref.at[m, x],
            w_send.at[m, k],
            w_recv.at[m, k],
            {"dp": 2 * x_at(k) + core},
        )

    def dw_in(k, m):
        spot = dw_recv_ref.at[m, x_at(-k)]
        return remote(
            spot, spot, w_send.at[m, k], w_recv.at[m, k], {"dp": 2 * x_at(k) + core}
        )

    put_dw(0, own_ref)
    pair(0).start()

    @pl.loop(1, ny)
    def _(k):
        term_y_in(k).wait_recv()

    total = back_slab_ref[0].astype(F32)
    for k in range(1, ny):
        total = total + back_slab_ref[k].astype(F32)
    back_sum_ref[...] = total.astype(BF16)

    @pl.loop(1, nz)
    def _(k):
        term_z(k).start()

    back_hubs_ref[at(z, hub), :] = back_sum_ref[at(z, hub), :]

    pair_sum(0)

    for i in range(height // lanes):
        count_ref[:, lanes * i : lanes * (i + 1)] = jnp.transpose(
            count_t_ref[lanes * i : lanes * (i + 1), :]
        )

    @pl.loop(0, rows // step)
    def _(i):
        span = at(i, step)
        grad_ref[span, :] = dtable(i * step) + dot(g_ref[span, :], ws_ref[...], TRANS)
        base_ref[span, :] = dot(own_ref[span, :], ws_ref[...])
        total_ref[span, :] = dot(count_ref[span, :rows], own_ref[...])

    down = lax.broadcasted_iota(jnp.int32, (rows, lanes), 0)
    for i in range(last + 1):
        spread_ref[:, lanes * i : lanes * (i + 1)] = (
            (idx_ref[i : i + 1, :] == down).astype(F32).astype(BF16)
        )

    @pl.loop(1, ny)
    def _(k):
        hub_y_in(k).wait_recv()

    @pl.loop(0, rows // step)
    def _(i):
        span = at(i, step)
        total_ref[span, :] += dot(count_ref[span, rows : rows + nhub], hubs_ref[...])

    near = [0]
    for k in range(1, nz // 2):
        near += [k, nz - k]
    near.append(nz // 2)
    plane = ny * cap
    def planes(pair_of, arrived, lhs_ref, start, rhs_ref):
        for dz in pair_of:

            @pl.loop(max(dz * ny, 1), (dz + 1) * ny)
            def _(k):
                arrived(k).wait_recv()

        at_z = [z_at(-dz) for dz in pair_of]
        c = [lhs_ref[:, pl.ds(pl.multiple_of(start + q * plane, plane), plane)] for q in at_z]
        r = [rhs_ref[at(q, plane), :] for q in at_z]
        return dot(jnp.concatenate(c, axis=1), jnp.concatenate(r, axis=0))

    turns = [near[i : i + 2] for i in range(0, nz, 2)]
    for turn in turns[:-1]:
        total_ref[...] += planes(turn, forth_in, count_ref, rows + nhub, recv_ref)
    total = total_ref[...] + planes(turns[-1], forth_in, count_ref, rows + nhub, recv_ref)
    agg_ref[...] = (total * by_vertex(slice(None))).astype(BF16)

    put_dw(1, agg_ref)
    pair(1).start()
    pair_sum(1)

    @pl.loop(0, rows // step)
    def _(i):
        span = at(i, step)
        out_ref[span, :] = (base_ref[span, :] + dot(agg_ref[span, :], wn_ref[...])).astype(BF16)

    for m in range(2):

        @pl.loop(1, nx)
        def _(k):
            dw_in(k, m).wait_recv()

        @pl.loop(0, parts)
        def _(q):
            total = dw_recv_ref[m, 0, q]
            for p in range(1, nx):
                total = total + dw_recv_ref[m, p, q]
            slab_ref[lax.rem(q, ny), q // ny, m] = total

    def slab_y(k):
        return to_y(k, slab_ref.at[y_at(k)], slab_recv_ref.at[y], sy_send, sy_recv)

    def slab_y_in(k):
        spot = slab_recv_ref.at[y_at(-k)]
        return to_y(k, spot, spot, sy_send, sy_recv)

    def ring(k):
        return to_z(k, ring_ref.at[z_at(k)], ring_recv_ref.at[z], sz_send, sz_recv)

    def ring_in(k):
        spot = ring_recv_ref.at[z_at(-k)]
        return to_z(k, spot, spot, sz_send, sz_recv)

    @pl.loop(1, ny)
    def _(k):
        slab_y(k).start()

    slab_recv_ref[y] = slab_ref[y]

    @pl.loop(1, ny)
    def _(k):
        slab_y_in(k).wait_recv()

    @pl.loop(0, nz)
    def _(q):
        total = slab_recv_ref[0, q]
        for p in range(1, ny):
            total = total + slab_recv_ref[p, q]
        ring_ref[q] = total

    @pl.loop(1, nz)
    def _(k):
        ring(k).start()

    ring_recv_ref[z] = ring_ref[z]

    @pl.loop(1, nz)
    def _(k):
        term_z_in(k).wait_recv()

    @pl.loop(0, rows // step)
    def _(i):
        span = at(i, step)
        grad_ref[span, :] += dot(spread_ref[span, sent:], back_hubs_ref[...])

    def finish_weights():
        @pl.loop(1, nz)
        def _(k):
            ring_in(k).wait_recv()

        total = ring_recv_ref[0]
        for q in range(1, nz):
            total = total + ring_recv_ref[q]
        fin_ref[...] = total * scale
        fin_recv_ref[lane] = fin_ref[...]

        @pl.loop(1, groups)
        def _(k):
            fin(k).start()

    def fin(k):
        return remote(
            fin_ref, fin_recv_ref.at[lane], e_send.at[k], e_recv.at[k], {"dp": d_at(k)}
        )

    def fin_in(k):
        spot = fin_recv_ref.at[d_at(-k)]
        return remote(spot, spot, e_send.at[k], e_recv.at[k], {"dp": d_at(k)})

    for turn in turns[:-1]:
        grad_ref[...] += planes(turn, back_in, spread_ref, 0, back_recv_ref)
    finish_weights()
    total = grad_ref[...] + planes(turns[-1], back_in, spread_ref, 0, back_recv_ref)
    gf_ref[...] = total.astype(BF16)

    @pl.loop(1, groups)
    def _(k):
        fin_in(k).wait_recv()

    for a in range(2):
        for b in range(width // lanes):
            here = (slice(8 * a, 8 * (a + 1)), slice(lanes * b, lanes * (b + 1)))
            gws_ref[here] = fin_recv_ref[4 * a + b, 0]
            gwn_ref[here] = fin_recv_ref[4 * a + b, 1]

    @pl.loop(1, parts)
    def _(k):
        forth(k).wait_send()
        back(k).wait_send()

    @pl.loop(1, nz)
    def _(k):
        hub_z(k).wait_send()
        term_z(k).wait_send()
        ring(k).wait_send()

    @pl.loop(1, ny)
    def _(k):
        hub_y(k).wait_send()
        term_y(k).wait_send()
        slab_y(k).wait_send()

    for m in range(2):
        pair(m).wait_send()

        @pl.loop(1, nx)
        def _(k):
            dw_copy(k, m).wait_send()

    @pl.loop(1, groups)
    def _(k):
        fin(k).wait_send()


def publish(*refs):
    for src, dst in zip(refs[:4], refs[4:]):
        dst[...] = src[...]


def shards(feats, grad_out, w_self, w_neigh, nbr, deg, hub_rows, send_rows):
    own = feats[0]
    rows, width = own.shape
    slots = nbr.shape[2]
    parts = lax.axis_size("graph")
    groups = lax.axis_size("dp")
    hub = hub_rows.shape[1]
    cap = send_rows.shape[3]
    sent = parts * cap
    nhub = parts * hub
    height = rows + nhub + sent
    ny = COLUMNS
    nz = parts // ny
    nx = groups // 2
    scale = float((groups * parts * rows) ** -0.5)
    vmem = pltpu.VMEM
    dma = pltpu.SemaphoreType.DMA
    outs = pl.pallas_call(
        functools.partial(layer_kernel, parts, groups, scale),
        out_shape=(
            jax.ShapeDtypeStruct((rows, width), BF16),
            jax.ShapeDtypeStruct((rows, width), BF16),
            jax.ShapeDtypeStruct((width // parts, width), F32),
            jax.ShapeDtypeStruct((width // parts, width), F32),
        ),
        in_specs=[pl.BlockSpec(memory_space=pl.ANY)] * 8,
        out_specs=[pl.BlockSpec(memory_space=vmem)] * 4,
        scratch_shapes=[
            vmem((rows, width), BF16),
            vmem((rows, width), BF16),
            vmem((width, width), BF16),
            vmem((width, width), BF16),
            vmem((slots, 1, rows), jnp.int32),
            vmem((1, rows), jnp.int32),
            vmem((parts, cap), jnp.int32),
            vmem((1, hub), jnp.int32),
            vmem((sent // 128 + 1, 128), jnp.int32),
            vmem((slots, rows), jnp.int32),
            vmem((sent + hub, rows), BF16),
            vmem((rows, sent + 128), BF16),
            vmem((height, rows), BF16),
            vmem((rows, height), BF16),
            vmem((sent, width), BF16),
            vmem((hub, width), BF16),
            vmem((sent, width), BF16),
            vmem((nhub, width), BF16),
            vmem((rows, width), BF16),
            vmem((rows, width), BF16),
            vmem((rows, width), F32),
            vmem((sent, width), BF16),
            vmem((nhub, width), BF16),
            vmem((sent, width), BF16),
            vmem((ny, nz * hub, width), BF16),
            vmem((nz * hub, width), BF16),
            vmem((nz * hub, width), BF16),
            vmem((rows, width), F32),
            vmem((rows, width), F32),
            vmem((rows, width), BF16),
            vmem((rows, 128), F32),
            vmem((2, 2, nx, parts, 8, 128), F32),
            vmem((2, nx, parts, 8, 128), F32),
            vmem((2, nx, parts, 8, 128), F32),
            vmem((ny, nz, 2, 8, 128), F32),
            vmem((ny, nz, 2, 8, 128), F32),
            vmem((nz, 2, 8, 128), F32),
            vmem((nz, 2, 8, 128), F32),
            vmem((2, 8, 128), F32),
            vmem((groups, 2, 8, 128), F32),
        ]
        + [dma((8,))]
        + [dma((parts,))] * 4
        + ([dma((nz,))] * 2 + [dma((ny,))] * 2)
        + ([dma((ny,))] * 2 + [dma((nz,))] * 2)
        + ([dma((2,))] * 2 + [dma((2, nx))] * 2)
        + ([dma((ny,))] * 2 + [dma((nz,))] * 2)
        + [dma((groups,))] * 2,
        compiler_params=pltpu.CompilerParams(collective_id=0, has_side_effects=True),
    )(
        own,
        grad_out[0],
        w_self,
        w_neigh,
        jnp.transpose(nbr, (2, 0, 1)),
        deg,
        send_rows[0, 0],
        hub_rows,
    )
    out, grad_feats, grad_w_self, grad_w_neigh = pl.pallas_call(
        publish,
        out_shape=tuple(jax.ShapeDtypeStruct(a.shape, a.dtype) for a in outs),
        in_specs=[pl.BlockSpec(memory_space=vmem)] * 4,
        out_specs=[pl.BlockSpec(memory_space=vmem)] * 4,
    )(*outs)
    return (out[None], grad_feats[None], grad_w_self, grad_w_neigh)


def solution(mesh):
    placed = (
        P("dp", "graph", None),
        P("dp", "graph", None),
        P(),
        P(),
        P("dp", "graph", None),
        P("dp", "graph"),
        P("dp", "graph"),
        P("dp", "graph", None, None),
    )
    return jax.shard_map(
        shards,
        mesh=mesh,
        in_specs=placed,
        out_specs=(
            P("dp", "graph", None),
            P("dp", "graph", None),
            P("graph", None),
            P("graph", None),
        ),
        check_vma=False,
    )
```
